512 devices in a mesh: row: 16 (over y, z_hi), col: 32 (over x, z_lo, core).
Axes of the slice: x: 4, y: 4, z: 16 (z_hi: 4, z_lo: 4; z = z_hi * 4 + z_lo), core: 2. Of those that a mesh axis runs over, the one named last changes fastest.
Arguments:
- inv_known: float32 [8192, 8192], P('row', 'col'), as said below
- pattern: int32 [128, 128], P('row', 'col'), may hold values from 0 to 1, as said below
- factor: float32 [8192, 2, 512], P(('row', 'col')), may hold values from -0.0625 to 0.0625
- listed: int32 [8192, 2], P(('row', 'col')), may hold values 0 or 1
- diag_inverse: float32 [512, 2, 512], P('col'), may hold values from -6 to 6
Outputs:
- inverse_columns: float32 [512, 2, 8192], P('col', None, 'row')
- schur: float32 [512, 2, 512], P('col')
The draws below stay inside these ranges and needn't reach their ends.
Inputs may be any that keep to these rules, and one draw needn't show every extreme that they name: `inv_known`: symmetric. `pattern`: symmetric; every diagonal tile is present.
All inputs are finite; a program needn't handle non-finite values. No bound on the sum of `listed` on one device may be relied on, other than what follows from the above.
Results may differ from the reference program's by a relative error of at most 0.0001.
Values sent between devices are 32-bit elements; how exact they have to be, the bound alone decides.
A program may use at most 64 MiB of HBM per device.

```python
import jax
import jax.numpy as jnp
from jax import lax

W = 512
KS = 2
TILE = 64
R = 8192
RT = 128
N_COL = 32


def draw_inv_known(key, part):
    values = jax.random.normal(key, (R, R), jnp.float32)
    return (values + values.T) * 0.70710678


def draw_pattern(key, part):
    score = jax.random.randint(key, (RT, RT), 0, 5)
    upper = jnp.where(score < 3, 1, 0)
    index = jnp.arange(RT)
    mirrored = jnp.where(index[:, None] <= index[None, :], upper, upper.T)
    return jnp.where(index[:, None] == index[None, :], 1, mirrored).astype(jnp.int32)


def with_ends(drawn, stream_key, low, high):
    extent = drawn.shape
    spot = [jax.random.randint(jax.random.fold_in(stream_key, axis), (), 0, extent[axis]) for axis in range(len(extent))]
    drawn = drawn.at[tuple(spot)].set(low)
    longest = extent.index(max(extent))
    spot[longest] = (spot[longest] + 1) % extent[longest]
    return drawn.at[tuple(spot)].set(high)


def level_of(rng, dims, split, low, top_value):
    factor_of = 1.0
    for dim, parts in split:
        heights = jax.random.uniform(jax.random.fold_in(jax.random.fold_in(rng, 6), dim), (parts,), jnp.float32, low / len(split), top_value / len(split))
        factor_of = factor_of * jnp.repeat(jnp.exp(heights), dims[dim] // parts).reshape((-1,) + (1,) * (len(dims) - 1 - dim))
    return factor_of


def centred(stream_key, extent, scale, bound, split=(), kind=jnp.bfloat16):
    result = scale * jax.random.normal(stream_key, extent, jnp.float32)
    if split:
        result = result * level_of(stream_key, extent, split, -0.22, 0.18)
    return jnp.clip(result, -bound, bound).astype(kind)


def setup_inputs(seed: int = 0) -> dict:
    splits = jax.random.split(jax.random.key(seed), 6)
    return {
        "inv_known": draw_inv_known(jax.random.fold_in(splits[5], 71), 0),
        "pattern": draw_pattern(jax.random.fold_in(splits[5], 71), 0),
        "factor": centred(splits[2], (R, KS, W), R ** -0.5, 0.0625, ((0, 512),), jnp.float32),
        "listed": with_ends((jax.random.randint(splits[3], (R, KS), 0, 4) < 3).astype(jnp.int32), jax.random.fold_in(splits[3], 1), 0, 1),
        "diag_inverse": centred(splits[4], (W, KS, W), 1.0, 6.0, ((0, 32),), jnp.float32),
    }


def reference(inv_known, pattern, factor, listed, diag_inverse):
    listed_f = listed.astype(jnp.float32)
    masked = factor * listed_f[:, :, None]
    flat = masked.reshape(R, KS * W)
    width = R // N_COL
    tiles = width // TILE

    def add_block(total, index):
        start = index * width
        cols = lax.dynamic_slice_in_dim(inv_known, start, width, 1)
        flags = lax.dynamic_slice_in_dim(pattern, index * tiles, tiles, 1).astype(jnp.float32)
        spread = jnp.repeat(jnp.repeat(flags, TILE, axis=0), TILE, axis=1)
        rows = lax.dynamic_slice_in_dim(flat, start, width, 0)
        part = jnp.dot(cols * spread, rows, precision=lax.Precision.HIGHEST, preferred_element_type=jnp.float32)
        return total + part, None

    init = jnp.zeros((R, KS * W), jnp.float32)
    total, _ = lax.scan(add_block, init, jnp.arange(N_COL, dtype=jnp.int32))
    columns = -total.reshape(R, KS, W) * listed_f[:, :, None]
    inverse_columns = jnp.transpose(columns, (2, 1, 0))
    update = jnp.einsum("ika,ikb->akb", columns, masked, precision=lax.Precision.HIGHEST)
    schur = diag_inverse - update
    return inverse_columns, schur
```

```python
import jax
import jax.numpy as jnp
from jax import lax
from jax.experimental import pallas as pl
from jax.experimental.pallas import tpu as pltpu
from jax.sharding import PartitionSpec as P

MESH = pl.DeviceIdType.MESH
F32 = jnp.float32
BF16 = jnp.bfloat16

S = 4
ROWS = 16
KS = 2
LANES = 128
GR = S * ROWS + 8


def mod(v):
    return lax.rem(v, S)


def split(v):
    hi = v.astype(BF16)
    return hi, (v - hi.astype(F32)).astype(BF16)


def dot3(ah, al, bh, bl):
    def dot(a, b):
        return jnp.dot(a, b, preferred_element_type=F32)

    return dot(ah, bh) + (dot(ah, bl) + dot(al, bh))


def kernel(
    inv_ref, pat_ref, fac_ref, lst_ref, dia_ref, col_ref, sch_ref,
    ph, plo, gat, mh, ml, tq, yb, zt, rb, ub, yu, zv, fw,
    g_send, g_recv, y_send, y_recv, z_send, z_recv,
    u_send, u_recv, v_send, v_recv, w_send, w_recv,
):
    r, c = lax.axis_index("row"), lax.axis_index("col")
    y, h = lax.div(r, S), lax.rem(r, S)
    x, z, core = lax.div(c, 2 * S), lax.rem(lax.div(c, 2), S), lax.rem(c, 2)
    sib = 1 - core

    def rid(yy, hh):
        return yy * S + hh

    def cid(xx, zz, cc):
        return (xx * S + zz) * 2 + cc

    def quarter(xx, yy):
        return mod(2 * xx + S - yy)

    mine = quarter(x, y)
    alone = jnp.logical_and(x == y, z == h)

    barrier = pltpu.get_barrier_semaphore()

    def greet(rr, cc):
        pl.semaphore_signal(barrier, inc=1, device_id=(rr, cc), device_id_type=MESH)

    greet(r, cid(x, z, sib))
    for d in (1, 2, 3):
        greet(r, cid(x, mod(z + d), core))
        greet(rid(mod(y + d), h), c)
        greet(rid(y, mod(h + d)), c)
    greet(r, cid(mod(x + 1), z, core))
    greet(r, cid(mod(x + 3), z, core))
    for hs in range(S):
        for cs in range(2):
            rr, cc = rid(quarter(y, x), hs), cid(y, h, cs)

            @pl.when(jnp.logical_or(rr != r, cc != c))
            def _():
                greet(rr, cc)

    listed = lst_ref[...].astype(F32)
    lane = lax.broadcasted_iota(jnp.int32, (ROWS, LANES), 1)
    row = lax.broadcasted_iota(jnp.int32, (ROWS, LANES), 0)
    spot = lane == row + lax.rem(c, LANES // ROWS) * ROWS
    for k in range(KS):
        flag = listed[:, k : k + 1]
        rows = fac_ref[:, k, :] * flag
        for b in range(S):
            gat[c, k, b * ROWS : (b + 1) * ROWS, :] = rows[:, b * LANES : (b + 1) * LANES]
        line = jnp.sum(jnp.where(spot, flag, 0.0), axis=0, keepdims=True)
        gat[c, k, S * ROWS :, :] = jnp.broadcast_to(line, (8, LANES))

    flags = pat_ref[...].astype(F32)
    tcol = lax.div(lax.broadcasted_iota(jnp.int32, (8, 256), 1), 64)
    wide = jnp.zeros((8, 256), F32)
    for t in range(4):
        wide = jnp.where(tcol == t, flags[:, t : t + 1], wide)
    for g in range(4):
        block = jnp.concatenate(
            [inv_ref[(2 * g + e) * 64 : (2 * g + e + 1) * 64, :] * wide[2 * g + e : 2 * g + e + 1, :] for e in range(2)],
            axis=0,
        )
        hi, lo = split(block.T)
        ph[:, g * 128 : (g + 1) * 128] = hi
        plo[:, g * 128 : (g + 1) * 128] = lo

    pl.semaphore_wait(barrier, 20 - alone.astype(jnp.int32))

    sends = []

    def send(src, dst, ssem, rsem, rr, cc):
        copy = pltpu.make_async_remote_copy(
            src_ref=src, dst_ref=dst, send_sem=ssem, recv_sem=rsem, device_id=(rr, cc), device_id_type=MESH
        )
        copy.start()
        sends.append(copy)

    def arrive(dst, rsem):
        pltpu.make_async_copy(dst, dst, rsem).wait()

    count = [0] * KS

    def pass_on(k, cs, cc):
        shard = gat.at[cs, k]
        send(shard, shard, g_send.at[k, count[k]], g_recv.at[k, cs], r, cc)
        count[k] += 1

    def got(k, cs):
        arrive(gat.at[cs, k], g_recv.at[k, cs])

    right, left = cid(mod(x + 1), z, core), cid(mod(x + 3), z, core)
    partner = cid(x, z, sib)

    def start_gather(k):
        for cc in (right, left, cid(x, mod(z + 1), core), cid(x, mod(z + 3), core), cid(x, mod(z + 2), core), partner):
            pass_on(k, c, cc)

    def line_gather(k):
        got(k, left)
        pass_on(k, left, right)
        pass_on(k, left, partner)
        got(k, right)
        pass_on(k, right, partner)
        for d in (1, 3, 2):
            cs = cid(x, mod(z + d), core)
            got(k, cs)
            for cc in (right, left, partner):
                pass_on(k, cs, cc)

    def finish_gather(k):
        for d in (1, 3, 2):
            cs = cid(mod(x + 3), mod(z + d), core)
            got(k, cs)
            if d == 1:
                pass_on(k, cs, right)
            pass_on(k, cs, partner)
            cs = cid(mod(x + 1), mod(z + d), core)
            got(k, cs)
            if d != 1:
                pass_on(k, cs, left)
            pass_on(k, cs, partner)
        for d in range(S):
            cs = cid(mod(x + 2), mod(z + d), core)
            got(k, cs)
            pass_on(k, cs, partner)
        for xx in range(S):
            for zz in range(S):
                got(k, cid(xx, zz, sib))

    def product(k):
        for b in range(0, S, 2):
            block = jnp.concatenate(
                [gat[:, k, e * ROWS : (e + 1) * ROWS, :].reshape(32 * ROWS, LANES) for e in (b, b + 1)], axis=1
            )
            bh, bl = split(block)
            mh[k, :, b * LANES : (b + 2) * LANES] = bh
            ml[k, :, b * LANES : (b + 2) * LANES] = bl
            t = dot3(ph[...], plo[...], bh, bl)
            tq[k, b] = t[:, :LANES]
            tq[k, b + 1] = t[:, LANES:]
        for d in (1, 3, 2):
            yy = mod(y + d)
            send(tq.at[k, quarter(x, yy)], yb.at[k, d], y_send.at[k, d], y_recv.at[k, d], rid(yy, h), c)

    def to_owner(k):
        for d in (1, 3, 2):
            arrive(yb.at[k, d], y_recv.at[k, d])
        total = (tq[k, mine] + yb[k, 1]) + (yb[k, 2] + yb[k, 3])
        zt[k] = total.T.reshape(8, ROWS, 256)
        for t in range(S):
            for cc in range(2):
                rr, ct, e = rid(x, z), cid(mine, t, cc), t * 2 + cc
                here = jnp.logical_and(rr == r, ct == c)

                @pl.when(here)
                def _():
                    pltpu.make_async_copy(zt.at[k, e], rb.at[k, h, core], z_recv.at[k, h, core]).start()

                @pl.when(jnp.logical_not(here))
                def _():
                    pltpu.make_async_remote_copy(
                        src_ref=zt.at[k, e], dst_ref=rb.at[k, h, core], send_sem=z_send.at[k, e],
                        recv_sem=z_recv.at[k, h, core], device_id=(rr, ct), device_id_type=MESH,
                    ).start()

    def sent_to_owner(k):
        for t in range(S):
            for cc in range(2):
                rr, ct, e = rid(x, z), cid(mine, t, cc), t * 2 + cc

                @pl.when(jnp.logical_or(rr != r, ct != c))
                def _():
                    pltpu.make_async_copy(zt.at[k, e], zt.at[k, e], z_send.at[k, e]).wait()

    def update(k):
        for hs in range(S):
            for cs in range(2):
                arrive(rb.at[k, hs, cs], z_recv.at[k, hs, cs])
        parts = rb[k]
        total = (parts[0] + parts[1]) + (parts[2] + parts[3])
        total = jnp.concatenate([total[0], total[1]], axis=1)
        line = jnp.concatenate(
            [jnp.sum(gat[8 * b : 8 * b + 8, k, S * ROWS :, :], axis=0)[0:1, :] for b in range(S)], axis=1
        )
        columns = -total * line
        col_ref[:, k, :] = columns
        ch, cl = split(columns)
        u = dot3(ch, cl, mh[k], ml[k])
        for q in range(S):
            ub[k, q] = u[:, q * LANES : (q + 1) * LANES]
        for d in (1, 3, 2):
            yy = mod(y + d)
            send(ub.at[k, yy], yu.at[k, d], u_send.at[k, d], u_recv.at[k, d], rid(yy, h), c)

    def across(k):
        for d in (1, 3, 2):
            arrive(yu.at[k, d], u_recv.at[k, d])
        zv[k, h] = (ub[k, y] + yu[k, 1]) + (yu[k, 2] + yu[k, 3])
        for d in (2, 1, 3):
            send(zv.at[k, h], zv.at[k, h], v_send.at[k, d], v_recv.at[k, d], rid(y, mod(h + d)), c)

    def back(k):
        for d in (1, 3, 2):
            hs = mod(h + S - d)
            arrive(zv.at[k, hs], v_recv.at[k, d])
        fw[k, y] = (zv[k, 0] + zv[k, 1]) + (zv[k, 2] + zv[k, 3])
        for d in (2, 1, 3):
            send(fw.at[k, y], fw.at[k, y], w_send.at[k, d], w_recv.at[k, d], rid(mod(y + d), h), c)

    def finish(k):
        for d in (1, 3, 2):
            ys = mod(y + S - d)
            arrive(fw.at[k, ys], w_recv.at[k, d])
        for q in range(S):
            at = slice(q * LANES, (q + 1) * LANES)
            sch_ref[:, k, at] = dia_ref[:, k, at] - fw[k, q]

    start_gather(0)
    line_gather(0)
    start_gather(1)
    finish_gather(0)
    product(0)
    line_gather(1)
    finish_gather(1)
    product(1)
    to_owner(0)
    to_owner(1)
    update(0)
    across(0)
    update(1)
    across(1)
    back(0)
    back(1)
    finish(0)
    finish(1)
    for copy in sends:
        copy.wait_send()
    sent_to_owner(0)
    sent_to_owner(1)


def local(inv_known, pattern, factor, listed, diag_inverse):
    width = diag_inverse.shape[0]
    vmem = pl.BlockSpec(memory_space=pltpu.VMEM)
    dma = pltpu.SemaphoreType.DMA
    out = jax.ShapeDtypeStruct((width, KS, 512), F32)
    return pl.pallas_call(
        kernel,
        out_shape=(out, out),
        in_specs=[vmem] * 5,
        out_specs=(vmem, vmem),
        scratch_shapes=[
            pltpu.VMEM((256, 512), BF16),
            pltpu.VMEM((256, 512), BF16),
            pltpu.VMEM((32, KS, GR, LANES), F32),
            pltpu.VMEM((KS, 512, 512), BF16),
            pltpu.VMEM((KS, 512, 512), BF16),
            pltpu.VMEM((KS, S, 256, LANES), F32),
            pltpu.VMEM((KS, S, 256, LANES), F32),
            pltpu.VMEM((KS, 8, ROWS, 256), F32),
            pltpu.VMEM((KS, S, 2, ROWS, 256), F32),
            pltpu.VMEM((KS, S, ROWS, LANES), F32),
            pltpu.VMEM((KS, S, ROWS, LANES), F32),
            pltpu.VMEM((KS, S, ROWS, LANES), F32),
            pltpu.VMEM((KS, S, ROWS, LANES), F32),
            dma((KS, 31)), dma((KS, 32)),
            dma((KS, S)), dma((KS, S)),
            dma((KS, 8)), dma((KS, S, 2)),
            dma((KS, S)), dma((KS, S)),
            dma((KS, S)), dma((KS, S)),
            dma((KS, S)), dma((KS, S)),
        ],
        compiler_params=pltpu.CompilerParams(collective_id=0, has_side_effects=True),
    )(inv_known, pattern, factor, listed, diag_inverse)


def solution(mesh):
    in_specs = (
        P("row", "col"),
        P("row", "col"),
        P(("row", "col"), None, None),
        P(("row", "col"), None),
        P("col", None, None),
    )
    out_specs = (P("col", None, "row"), P("col", None, None))
    return jax.shard_map(local, mesh=mesh, in_specs=in_specs, out_specs=out_specs, check_vma=False)
```

```python
import jax
import jax.numpy as jnp
from jax import lax
from jax.experimental import pallas as pl
from jax.experimental.pallas import tpu as pltpu
from jax.sharding import PartitionSpec as P

MESH = pl.DeviceIdType.MESH
F32 = jnp.float32
BF16 = jnp.bfloat16

S = 4
ROWS = 16
KS = 2
LANES = 128
PART = 32
CHUNKS = 4
HEAD = 8
GR = HEAD + CHUNKS * 2 * ROWS


def mod(v):
    return lax.rem(v, S)


def split(v):
    hi = v.astype(BF16)
    return hi, (v - hi.astype(F32)).astype(BF16)


def dot3(ah, al, bh, bl):
    def dot(a, b):
        return jnp.dot(a, b, preferred_element_type=F32)

    return dot(ah, bh) + (dot(ah, bl) + dot(al, bh))


def regroup(v):
    blocks = []
    for t in range(S):
        blocks += [v[:, q * LANES + t * PART : q * LANES + (t + 1) * PART] for q in range(S)]
    return jnp.concatenate(blocks, axis=1)


def kernel(
    inv_ref, pat_ref, fac_ref, lst_ref, col_ref, sch_ref,
    inv, ph, plo, gat, mh, ml, tq, yb, zt, rb, ub, yu, zv, fw,
    i_sem, far_sem, g_send, g_recv, y_send, y_recv, z_send, z_recv,
    u_send, u_recv, v_send, v_recv, w_send, w_recv,
):
    r, c = lax.axis_index("row"), lax.axis_index("col")
    y, h = lax.div(r, S), lax.rem(r, S)
    x, z, core = lax.div(c, 2 * S), lax.rem(lax.div(c, 2), S), lax.rem(c, 2)
    sib = 1 - core

    def rid(yy, hh):
        return yy * S + hh

    def cid(xx, zz, cc):
        return (xx * S + zz) * 2 + cc

    def quarter(xx, yy):
        return mod(2 * xx + S - yy)

    mine = quarter(x, y)
    line = (z + 1 - 2 * lax.rem(z, 2), jnp.where(z < 2, 2, 1), jnp.where(z < 2, 3, 0))
    right, left, partner = cid(mod(x + 1), z, core), cid(mod(x + 3), z, core), cid(x, z, sib)
    across_x = cid(mod(x + 2), z, core)

    barrier = pltpu.get_barrier_semaphore()

    def greet(sem, rr, cc):
        pl.semaphore_signal(sem, inc=1, device_id=(rr, cc), device_id_type=MESH)

    greet(barrier, rid(y, mod(h + 1)), c)
    greet(barrier, rid(y, mod(h + 3)), c)
    for zz in line:
        greet(barrier, r, cid(x, zz, core))
    for d in (2, 1, 3):
        greet(barrier, rid(mod(y + d), h), c)
    for cc in (right, left, across_x, partner):
        greet(barrier, r, cc)

    load = pltpu.make_async_copy(inv_ref, inv, i_sem)
    load.start()

    listed = lst_ref[...].astype(F32)
    eye = lax.broadcasted_iota(jnp.int32, (ROWS, ROWS), 0) == lax.broadcasted_iota(jnp.int32, (ROWS, ROWS), 1)
    lane = lax.broadcasted_iota(jnp.int32, (ROWS, LANES), 1)
    row = lax.broadcasted_iota(jnp.int32, (ROWS, LANES), 0)
    spot = lane == row + lax.rem(c, LANES // ROWS) * ROWS
    lines = []
    for k in range(KS):
        flag = jnp.sum(jnp.where(eye, listed[k : k + 1, :], 0.0), axis=1, keepdims=True)
        rows = regroup(fac_ref[:, k, :] * flag)
        for t in range(S):
            at = HEAD + (k * S + t) * ROWS
            gat[c, at : at + ROWS, :] = rows[:, t * LANES : (t + 1) * LANES]
        lines.append(jnp.sum(jnp.where(spot, flag, 0.0), axis=0, keepdims=True))
    which = lax.broadcasted_iota(jnp.int32, (HEAD, LANES), 0) == 0
    gat[c, :HEAD, :] = jnp.where(which, lines[0], lines[1])

    pl.semaphore_wait(barrier, 12)

    rounds = (
        [(rid(y, mod(h + 1)), c), (rid(y, mod(h + 3)), c)],
        [(rid(mod(y + d), h), c) for d in (2, 1, 3)],
        [(r, cid(x, zz, core)) for zz in line],
        [(r, right), (r, left), (r, across_x)],
        [(r, partner)],
    )

    def tell(n):
        for rr, cc in rounds[n]:
            greet(far_sem.at[n], rr, cc)

    def heard(n):
        pl.semaphore_wait(far_sem.at[n], len(rounds[n]))
        if n + 1 < len(rounds):
            tell(n + 1)

    tell(0)

    sends = []

    def copy(src, dst, ssem, rsem, rr, cc):
        return pltpu.make_async_remote_copy(
            src_ref=src, dst_ref=dst, send_sem=ssem, recv_sem=rsem, device_id=(rr, cc), device_id_type=MESH
        )

    def send(*args):
        it = copy(*args)
        it.start()
        sends.append(it)

    def arrive(dst, sem):
        pltpu.make_async_copy(dst, dst, sem).wait()

    def span(n):
        first = 0 if n == 0 else HEAD + n * 2 * ROWS
        return pl.ds(first, HEAD + (n + 1) * 2 * ROWS - first)

    def pass_on(n, cs, *to):
        shard = gat.at[cs, span(n)]
        for cc in to:
            copy(shard, shard, g_send.at[n], g_recv.at[n, cs], r, cc).start()

    def got(n, cs):
        arrive(gat.at[cs, span(n)], g_recv.at[n, cs])

    def start_gather(n):
        pass_on(n, c, right, left, cid(x, line[2], core), cid(x, line[1], core), cid(x, line[0], core), partner)

    def line_gather(n):
        got(n, left)
        pass_on(n, left, right, partner)
        got(n, right)
        pass_on(n, right, partner)
        for zz in line:
            cs = cid(x, zz, core)
            got(n, cs)
            pass_on(n, cs, right, left, partner)

    def relay_gather(n):
        for e, zz in enumerate(line):
            cs = cid(mod(x + 3), zz, core)
            got(n, cs)
            if e == 0:
                pass_on(n, cs, right)
            pass_on(n, cs, partner)
            cs = cid(mod(x + 1), zz, core)
            got(n, cs)
            if e != 0:
                pass_on(n, cs, left)
            pass_on(n, cs, partner)

    def finish_gather(n):
        for zz in (z, *line):
            cs = cid(mod(x + 2), zz, core)
            got(n, cs)
            pass_on(n, cs, partner)
        for cs in range(S * S):
            got(n, 2 * cs + sib)

    def gathered(n):
        shards = gat.at[pl.ds(0, 31), span(n)]
        pltpu.make_async_copy(shards, shards, g_send.at[n]).wait()

    def prepare():
        flags = pat_ref[...].astype(F32)
        tile = lax.div(lax.broadcasted_iota(jnp.int32, (S, 512), 1), 64)
        wide = jnp.zeros((S, 512), F32)
        for e in range(8):
            wide = jnp.where(tile == e, flags[:, e : e + 1], wide)
        load.wait()
        for g in range(4):
            at = slice(g * LANES, (g + 1) * LANES)
            mask = jnp.concatenate([jnp.broadcast_to(wide[t : t + 1, at], (64, LANES)) for t in range(S)], axis=0)
            hi, lo = split(inv[at, :].T * mask)
            ph[:, at] = hi
            plo[:, at] = lo

    def product(n):
        k, p = n // 2, n % 2
        at = HEAD + n * 2 * ROWS
        block = jnp.concatenate(
            [gat[:, at + e * ROWS : at + (e + 1) * ROWS, :].reshape(32 * ROWS, LANES) for e in range(2)], axis=1
        )
        bh, bl = split(block)
        mh[k, :, p * 256 : (p + 1) * 256] = bh
        ml[k, :, p * 256 : (p + 1) * 256] = bl
        t = dot3(ph[...], plo[...], bh, bl).T
        for e in range(2):
            for q in range(S):
                at = (e * S + q) * PART
                tq[n, q, e] = t[at : at + PART]
        for d in (2, 1, 3):
            yy = mod(y + d)
            send(tq.at[n, quarter(x, yy)], yb.at[n, d], y_send.at[n, d], y_recv.at[n, d], rid(yy, h), c)

    def owners(n):
        for e in range(2):
            for cc in range(2):
                yield e * 2 + cc, rid(x, z), cid(mine, (n % 2) * 2 + e, cc)

    def to_owner(n):
        k = n // 2
        for d in (1, 3, 2):
            arrive(yb.at[n, d], y_recv.at[n, d])
        total = (tq[n, mine] + yb[n, 1]) + (yb[n, 2] + yb[n, 3])
        zt[n] = total.reshape(4, ROWS, 256)
        for e, rr, ct in owners(n):
            here = jnp.logical_and(rr == r, ct == c)

            @pl.when(here)
            def _():
                pltpu.make_async_copy(zt.at[n, e], rb.at[k, h, core], z_recv.at[k, h, core]).start()

            @pl.when(jnp.logical_not(here))
            def _():
                copy(zt.at[n, e], rb.at[k, h, core], z_send.at[n, e], z_recv.at[k, h, core], rr, ct).start()

    def sent_to_owner(n):
        for e, rr, ct in owners(n):

            @pl.when(jnp.logical_or(rr != r, ct != c))
            def _():
                pltpu.make_async_copy(zt.at[n, e], zt.at[n, e], z_send.at[n, e]).wait()

    def update(k):
        marks = jnp.concatenate(
            [jnp.sum(gat[8 * b : 8 * b + 8, :HEAD, :], axis=0)[k : k + 1, :] for b in range(S)], axis=1
        )
        for hs in range(S):
            for cs in range(2):
                arrive(rb.at[k, hs, cs], z_recv.at[k, hs, cs])
        parts = rb[k]
        total = (parts[0] + parts[1]) + (parts[2] + parts[3])
        total = jnp.concatenate([total[0], total[1]], axis=1) * marks
        col_ref[:, k, :] = total
        ch, cl = split(total)
        u = regroup(dot3(ch, cl, mh[k], ml[k]))
        for q in range(S):
            ub[k, q] = u[:, q * LANES : (q + 1) * LANES]
        for d in (2, 1, 3):
            yy = mod(y + d)
            send(ub.at[k, yy], yu.at[k, d], u_send.at[k, d], u_recv.at[k, d], rid(yy, h), c)

    def across(k):
        for d in (1, 3, 2):
            arrive(yu.at[k, d], u_recv.at[k, d])
        zv[k, h] = (ub[k, y] + yu[k, 1]) + (yu[k, 2] + yu[k, 3])
        for d in (2, 1, 3):
            send(zv.at[k, h], zv.at[k, h], v_send.at[k, d], v_recv.at[k, d], rid(y, mod(h + d)), c)

    def back(k):
        for d in (1, 3, 2):
            hs = mod(h + S - d)
            arrive(zv.at[k, hs], v_recv.at[k, d])
        fw[k, y] = (zv[k, 0] + zv[k, 1]) + (zv[k, 2] + zv[k, 3])
        for d in (2, 1, 3):
            send(fw.at[k, y], fw.at[k, y], w_send.at[k, d], w_recv.at[k, d], rid(mod(y + d), h), c)

    def finish(k):
        for d in (1, 3, 2):
            ys = mod(y + S - d)
            arrive(fw.at[k, ys], w_recv.at[k, d])
        for q in range(S):
            sch_ref[:, k, q * LANES : (q + 1) * LANES] = fw[k, q]

    start_gather(0)
    start_gather(1)
    prepare()
    line_gather(0)
    heard(0)
    start_gather(2)
    line_gather(1)
    heard(1)
    relay_gather(0)
    heard(2)
    start_gather(3)
    line_gather(2)
    heard(3)
    finish_gather(0)
    product(0)
    heard(4)
    relay_gather(1)
    line_gather(3)
    finish_gather(1)
    product(1)
    to_owner(0)
    relay_gather(2)
    finish_gather(2)
    product(2)
    to_owner(1)
    relay_gather(3)
    finish_gather(3)
    product(3)
    to_owner(2)
    to_owner(3)
    for n in range(CHUNKS):
        gathered(n)
    update(0)
    across(0)
    update(1)
    across(1)
    back(0)
    back(1)
    finish(0)
    finish(1)
    for it in sends:
        it.wait_send()
    for n in range(CHUNKS):
        sent_to_owner(n)


def local(inv_known, pattern, factor, listed, diag_inverse):
    width = diag_inverse.shape[0]
    vmem = pl.BlockSpec(memory_space=pltpu.VMEM)
    dma = pltpu.SemaphoreType.DMA
    out = jax.ShapeDtypeStruct((width, KS, 512), F32)
    sums, total = pl.pallas_call(
        kernel,
        out_shape=(out, out),
        in_specs=[pl.BlockSpec(memory_space=pl.ANY), vmem, vmem, vmem],
        out_specs=(vmem, vmem),
        scratch_shapes=[
            pltpu.VMEM((512, 256), F32),
            pltpu.VMEM((256, 512), BF16),
            pltpu.VMEM((256, 512), BF16),
            pltpu.VMEM((32, GR, LANES), F32),
            pltpu.VMEM((KS, 512, 512), BF16),
            pltpu.VMEM((KS, 512, 512), BF16),
            pltpu.VMEM((CHUNKS, S, 2, PART, 256), F32),
            pltpu.VMEM((CHUNKS, S, 2, PART, 256), F32),
            pltpu.VMEM((CHUNKS, 4, ROWS, 256), F32),
            pltpu.VMEM((KS, S, 2, ROWS, 256), F32),
            pltpu.VMEM((KS, S, ROWS, LANES), F32),
            pltpu.VMEM((KS, S, ROWS, LANES), F32),
            pltpu.VMEM((KS, S, ROWS, LANES), F32),
            pltpu.VMEM((KS, S, ROWS, LANES), F32),
            dma(()), pltpu.SemaphoreType.REGULAR((5,)),
            dma((CHUNKS,)), dma((CHUNKS, 32)),
            dma((CHUNKS, S)), dma((CHUNKS, S)),
            dma((CHUNKS, 4)), dma((KS, S, 2)),
            dma((KS, S)), dma((KS, S)),
            dma((KS, S)), dma((KS, S)),
            dma((KS, S)), dma((KS, S)),
        ],
        compiler_params=pltpu.CompilerParams(collective_id=0, has_side_effects=True),
    )(inv_known, pattern.T, factor, listed.T)
    return -sums, diag_inverse + total


def solution(mesh):
    in_specs = (
        P("row", "col"),
        P("row", "col"),
        P(("row", "col"), None, None),
        P(("row", "col"), None),
        P("col", None, None),
    )
    out_specs = (P("col", None, "row"), P("col", None, None))
    return jax.shard_map(local, mesh=mesh, in_specs=in_specs, out_specs=out_specs, check_vma=False)
```

```python
import jax
import jax.numpy as jnp
from jax import lax
from jax.experimental import pallas as pl
from jax.experimental.pallas import tpu as pltpu
from jax.sharding import PartitionSpec as P

MESH = pl.DeviceIdType.MESH
F32 = jnp.float32
BF16 = jnp.bfloat16

S = 4
ROWS = 16
KS = 2
LANES = 128
PART = 32
CUTS = (0, 1, 2, 4, 6, 8)
CHUNKS = len(CUTS) - 1
DIRECT = (0, 1, 2, 3, 4)
HEAD = 8
GR = HEAD + KS * S * ROWS


def mod(v):
    return lax.rem(v, S)


def split(v):
    hi = v.astype(BF16)
    return hi, (v - hi.astype(F32)).astype(BF16)


def dot3(ah, al, bh, bl):
    def dot(a, b):
        return jnp.dot(a, b, preferred_element_type=F32)

    return dot(ah, bh) + (dot(ah, bl) + dot(al, bh))


def regroup(v):
    blocks = []
    for t in range(S):
        blocks += [v[:, q * LANES + t * PART : q * LANES + (t + 1) * PART] for q in range(S)]
    return jnp.concatenate(blocks, axis=1)


def kernel(
    inv_ref, pat_ref, fac_ref, lst_ref, col_ref, sch_ref,
    inv, ph, plo, gat, mh, ml, tq, yb, zt, rb, ub, yu, zv, fw,
    i_sem, far_sem, g_send, g_recv, y_send, y_recv, z_send, z_recv,
    u_send, u_recv, v_send, v_recv, w_send, w_recv,
):
    r, c = lax.axis_index("row"), lax.axis_index("col")
    y, h = lax.div(r, S), lax.rem(r, S)
    x, z, core = lax.div(c, 2 * S), lax.rem(lax.div(c, 2), S), lax.rem(c, 2)
    sib = 1 - core

    def rid(yy, hh):
        return yy * S + hh

    def cid(xx, zz, cc):
        return (xx * S + zz) * 2 + cc

    def quarter(xx, yy):
        return mod(2 * xx + S - yy)

    mine = quarter(x, y)
    line = (z + 1 - 2 * lax.rem(z, 2), jnp.where(z < 2, 2, 1), jnp.where(z < 2, 3, 0))
    right, left, partner = cid(mod(x + 1), z, core), cid(mod(x + 3), z, core), cid(x, z, sib)
    across_x = cid(mod(x + 2), z, core)

    barrier = pltpu.get_barrier_semaphore()

    def greet(sem, rr, cc):
        pl.semaphore_signal(sem, inc=1, device_id=(rr, cc), device_id_type=MESH)

    greet(barrier, rid(y, mod(h + 1)), c)
    greet(barrier, rid(y, mod(h + 3)), c)
    for zz in line:
        greet(barrier, r, cid(x, zz, core))
    for d in (2, 1, 3):
        greet(barrier, rid(mod(y + d), h), c)
    for cc in (right, left, across_x, partner):
        greet(barrier, r, cc)

    load = pltpu.make_async_copy(inv_ref, inv, i_sem)
    load.start()

    listed = lst_ref[...].astype(F32)
    eye = lax.broadcasted_iota(jnp.int32, (ROWS, ROWS), 0) == lax.broadcasted_iota(jnp.int32, (ROWS, ROWS), 1)
    lane = lax.broadcasted_iota(jnp.int32, (ROWS, LANES), 1)
    row = lax.broadcasted_iota(jnp.int32, (ROWS, LANES), 0)
    spot = lane == row + lax.rem(c, LANES // ROWS) * ROWS
    lines = []
    for k in range(KS):
        flag = jnp.sum(jnp.where(eye, listed[k : k + 1, :], 0.0), axis=1, keepdims=True)
        rows = regroup(fac_ref[:, k, :] * flag)
        for t in range(S):
            at = HEAD + (k * S + t) * ROWS
            gat[c, at : at + ROWS, :] = rows[:, t * LANES : (t + 1) * LANES]
        lines.append(jnp.sum(jnp.where(spot, flag, 0.0), axis=0, keepdims=True))
    which = lax.broadcasted_iota(jnp.int32, (HEAD, LANES), 0) == 0
    gat[c, :HEAD, :] = jnp.where(which, lines[0], lines[1])

    pl.semaphore_wait(barrier, 12)

    rounds = (
        [(rid(y, mod(h + 1)), c), (rid(y, mod(h + 3)), c)],
        [(rid(mod(y + d), h), c) for d in (2, 1, 3)],
        [(r, cid(x, zz, core)) for zz in line],
        [(r, right), (r, left), (r, across_x)],
        [(r, partner)],
    )

    def tell(n):
        for rr, cc in rounds[n]:
            greet(far_sem.at[n], rr, cc)

    def heard(n):
        pl.semaphore_wait(far_sem.at[n], len(rounds[n]))
        if n + 1 < len(rounds):
            tell(n + 1)

    tell(0)

    sends = []

    def copy(src, dst, ssem, rsem, rr, cc):
        return pltpu.make_async_remote_copy(
            src_ref=src, dst_ref=dst, send_sem=ssem, recv_sem=rsem, device_id=(rr, cc), device_id_type=MESH
        )

    def send(*args):
        it = copy(*args)
        it.start()
        sends.append(it)

    def arrive(dst, sem):
        pltpu.make_async_copy(dst, dst, sem).wait()

    def span(n):
        first = 0 if n == 0 else HEAD + CUTS[n] * ROWS
        return pl.ds(first, HEAD + CUTS[n + 1] * ROWS - first)

    def pass_on(n, cs, *to):
        shard = gat.at[cs, span(n)]
        for cc in to:
            copy(shard, shard, g_send.at[n], g_recv.at[n, cs], r, cc).start()

    def got(n, cs):
        arrive(gat.at[cs, span(n)], g_recv.at[n, cs])

    def opposite(n):
        return (across_x,) if n in DIRECT else ()

    def start_gather(n):
        pass_on(n, c, right, left, *opposite(n), cid(x, line[2], core), cid(x, line[1], core), cid(x, line[0], core), partner)

    def line_gather(n):
        got(n, left)
        pass_on(n, left, *([] if n in DIRECT else [right]), partner)
        got(n, right)
        pass_on(n, right, partner)
        for zz in line:
            cs = cid(x, zz, core)
            got(n, cs)
            pass_on(n, cs, right, left, *opposite(n), partner)

    def relay_gather(n):
        for e, zz in enumerate(line):
            cs = cid(mod(x + 3), zz, core)
            got(n, cs)
            if e == 0 and n not in DIRECT:
                pass_on(n, cs, right)
            pass_on(n, cs, partner)
            cs = cid(mod(x + 1), zz, core)
            got(n, cs)
            if e != 0 and n not in DIRECT:
                pass_on(n, cs, left)
            pass_on(n, cs, partner)

    def finish_gather(n):
        for zz in (z, *line):
            cs = cid(mod(x + 2), zz, core)
            got(n, cs)
            pass_on(n, cs, partner)
        for cs in range(S * S):
            got(n, 2 * cs + sib)

    def gathered(n):
        shards = gat.at[pl.ds(0, 31), span(n)]
        pltpu.make_async_copy(shards, shards, g_send.at[n]).wait()

    def prepare():
        flags = pat_ref[...].astype(F32)
        tile = lax.div(lax.broadcasted_iota(jnp.int32, (S, 512), 1), 64)
        wide = jnp.zeros((S, 512), F32)
        for e in range(8):
            wide = jnp.where(tile == e, flags[:, e : e + 1], wide)
        load.wait()
        for g in range(4):
            at = slice(g * LANES, (g + 1) * LANES)
            mask = jnp.concatenate([jnp.broadcast_to(wide[t : t + 1, at], (64, LANES)) for t in range(S)], axis=0)
            hi, lo = split(inv[at, :].T * mask)
            ph[:, at] = hi
            plo[:, at] = lo

    def blocks(n):
        return range(CUTS[n], CUTS[n + 1])

    def product(n):
        k, p = CUTS[n] // S, CUTS[n] % S
        cols = slice(p * LANES, p * LANES + len(blocks(n)) * LANES)
        rows = [gat[:, HEAD + b * ROWS : HEAD + (b + 1) * ROWS, :].reshape(32 * ROWS, LANES) for b in blocks(n)]
        bh, bl = split(jnp.concatenate(rows, axis=1))
        mh[k, :, cols] = bh
        ml[k, :, cols] = bl
        t = dot3(ph[...], plo[...], bh, bl).T
        for e, b in enumerate(blocks(n)):
            for q in range(S):
                at = (e * S + q) * PART
                tq[q, b] = t[at : at + PART]
        run = pl.ds(CUTS[n], len(blocks(n)))
        for d in (2, 1, 3):
            yy = mod(y + d)
            send(tq.at[quarter(x, yy), run], yb.at[d, run], y_send.at[n, d], y_recv.at[n, d], rid(yy, h), c)

    def owners(n):
        for b in blocks(n):
            for cc in range(2):
                yield b, cc, rid(x, z), cid(mine, b % S, cc)

    def to_owner(n):
        run = pl.ds(CUTS[n], len(blocks(n)))
        for d in (1, 3, 2):
            arrive(yb.at[d, run], y_recv.at[n, d])
        total = (tq[mine, run] + yb[1, run]) + (yb[2, run] + yb[3, run])
        zt[run] = total.reshape(len(blocks(n)), 2, ROWS, 256)
        for b, e, rr, ct in owners(n):
            k = b // S
            here = jnp.logical_and(rr == r, ct == c)

            @pl.when(here)
            def _():
                pltpu.make_async_copy(zt.at[b, e], rb.at[k, h, core], z_recv.at[k, h, core]).start()

            @pl.when(jnp.logical_not(here))
            def _():
                copy(zt.at[b, e], rb.at[k, h, core], z_send.at[b, e], z_recv.at[k, h, core], rr, ct).start()

    def sent_to_owner(n):
        for b, e, rr, ct in owners(n):

            @pl.when(jnp.logical_or(rr != r, ct != c))
            def _():
                pltpu.make_async_copy(zt.at[b, e], zt.at[b, e], z_send.at[b, e]).wait()

    def update(k):
        marks = jnp.concatenate(
            [jnp.sum(gat[8 * b : 8 * b + 8, :HEAD, :], axis=0)[k : k + 1, :] for b in range(S)], axis=1
        )
        for hs in range(S):
            for cs in range(2):
                arrive(rb.at[k, hs, cs], z_recv.at[k, hs, cs])
        parts = rb[k]
        total = (parts[0] + parts[1]) + (parts[2] + parts[3])
        total = jnp.concatenate([total[0], total[1]], axis=1) * marks
        col_ref[:, k, :] = total
        ch, cl = split(total)
        u = regroup(dot3(ch, cl, mh[k], ml[k]))
        for q in range(S):
            ub[k, q] = u[:, q * LANES : (q + 1) * LANES]
        for d in (2, 1, 3):
            yy = mod(y + d)
            send(ub.at[k, yy], yu.at[k, d], u_send.at[k, d], u_recv.at[k, d], rid(yy, h), c)

    def across(k):
        for d in (1, 3, 2):
            arrive(yu.at[k, d], u_recv.at[k, d])
        zv[k, h] = (ub[k, y] + yu[k, 1]) + (yu[k, 2] + yu[k, 3])
        for d in (2, 1, 3):
            send(zv.at[k, h], zv.at[k, h], v_send.at[k, d], v_recv.at[k, d], rid(y, mod(h + d)), c)

    def back(k):
        for d in (1, 3, 2):
            hs = mod(h + S - d)
            arrive(zv.at[k, hs], v_recv.at[k, d])
        fw[k, y] = (zv[k, 0] + zv[k, 1]) + (zv[k, 2] + zv[k, 3])
        for d in (2, 1, 3):
            send(fw.at[k, y], fw.at[k, y], w_send.at[k, d], w_recv.at[k, d], rid(mod(y + d), h), c)

    def finish(k):
        for d in (1, 3, 2):
            ys = mod(y + S - d)
            arrive(fw.at[k, ys], w_recv.at[k, d])
        for q in range(S):
            sch_ref[:, k, q * LANES : (q + 1) * LANES] = fw[k, q]

    start_gather(0)
    start_gather(1)
    start_gather(2)
    start_gather(3)
    start_gather(4)
    prepare()
    line_gather(0)
    heard(0)
    line_gather(1)
    heard(1)
    line_gather(2)
    heard(2)
    line_gather(3)
    heard(3)
    line_gather(4)
    relay_gather(0)
    finish_gather(0)
    heard(4)
    product(0)
    relay_gather(1)
    finish_gather(1)
    product(1)
    relay_gather(2)
    finish_gather(2)
    product(2)
    relay_gather(3)
    finish_gather(3)
    product(3)
    to_owner(0)
    to_owner(1)
    relay_gather(4)
    finish_gather(4)
    product(4)
    to_owner(2)
    to_owner(3)
    to_owner(4)
    for n in range(CHUNKS):
        gathered(n)
    update(0)
    across(0)
    update(1)
    across(1)
    back(0)
    back(1)
    finish(0)
    finish(1)
    for it in sends:
        it.wait_send()
    for n in range(CHUNKS):
        sent_to_owner(n)


def local(inv_known, pattern, factor, listed, diag_inverse):
    width = diag_inverse.shape[0]
    vmem = pl.BlockSpec(memory_space=pltpu.VMEM)
    dma = pltpu.SemaphoreType.DMA
    out = jax.ShapeDtypeStruct((width, KS, 512), F32)
    sums, total = pl.pallas_call(
        kernel,
        out_shape=(out, out),
        in_specs=[pl.BlockSpec(memory_space=pl.ANY), vmem, vmem, vmem],
        out_specs=(vmem, vmem),
        scratch_shapes=[
            pltpu.VMEM((512, 256), F32),
            pltpu.VMEM((256, 512), BF16),
            pltpu.VMEM((256, 512), BF16),
            pltpu.VMEM((32, GR, LANES), F32),
            pltpu.VMEM((KS, 512, 512), BF16),
            pltpu.VMEM((KS, 512, 512), BF16),
            pltpu.VMEM((S, KS * S, PART, 256), F32),
            pltpu.VMEM((S, KS * S, PART, 256), F32),
            pltpu.VMEM((KS * S, 2, ROWS, 256), F32),
            pltpu.VMEM((KS, S, 2, ROWS, 256), F32),
            pltpu.VMEM((KS, S, ROWS, LANES), F32),
            pltpu.VMEM((KS, S, ROWS, LANES), F32),
            pltpu.VMEM((KS, S, ROWS, LANES), F32),
            pltpu.VMEM((KS, S, ROWS, LANES), F32),
            dma(()), pltpu.SemaphoreType.REGULAR((5,)),
            dma((CHUNKS,)), dma((CHUNKS, 32)),
            dma((CHUNKS, S)), dma((CHUNKS, S)),
            dma((KS * S, 2)), dma((KS, S, 2)),
            dma((KS, S)), dma((KS, S)),
            dma((KS, S)), dma((KS, S)),
            dma((KS, S)), dma((KS, S)),
        ],
        compiler_params=pltpu.CompilerParams(collective_id=0, has_side_effects=True),
    )(inv_known, pattern.T, factor, listed.T)
    return -sums, diag_inverse + total


def solution(mesh):
    in_specs = (
        P("row", "col"),
        P("row", "col"),
        P(("row", "col"), None, None),
        P(("row", "col"), None),
        P("col", None, None),
    )
    out_specs = (P("col", None, "row"), P("col", None, None))
    return jax.shard_map(local, mesh=mesh, in_specs=in_specs, out_specs=out_specs, check_vma=False)
```

```python
import jax
import jax.numpy as jnp
from jax import lax
from jax.experimental import pallas as pl
from jax.experimental.pallas import tpu as pltpu
from jax.sharding import PartitionSpec as P

MESH = pl.DeviceIdType.MESH
F32 = jnp.float32
BF16 = jnp.bfloat16

S = 4
ROWS = 16
KS = 2
LANES = 128
PART = 32
CUTS = (0, 1, 2, 4, 6, 8)
CHUNKS = len(CUTS) - 1
ROUND = ()
HEAD = 8
GR = HEAD + KS * S * ROWS


def mod(v):
    return lax.rem(v, S)


def split(v):
    hi = v.astype(BF16)
    return hi, (v - hi.astype(F32)).astype(BF16)


def dot3(ah, al, bh, bl):
    def dot(a, b):
        return jnp.dot(a, b, preferred_element_type=F32)

    return dot(ah, bh) + (dot(ah, bl) + dot(al, bh))


def regroup(v):
    blocks = []
    for t in range(S):
        blocks += [v[:, q * LANES + t * PART : q * LANES + (t + 1) * PART] for q in range(S)]
    return jnp.concatenate(blocks, axis=1)


def kernel(
    inv_in, pat_in, fac_in, lst_in, col_ref, sch_ref,
    inv, pat_ref, fac_ref, lst_ref, ph, plo, gat, mh, ml, tq, yb, zt, rb, ub, yu, zv, fw,
    i_sem, far_sem, g_send, g_recv, y_send, y_recv, z_send, z_recv,
    u_send, u_recv, v_send, v_recv, w_send, w_recv,
):
    r, c = lax.axis_index("row"), lax.axis_index("col")
    y, h = lax.div(r, S), lax.rem(r, S)
    x, z, core = lax.div(c, 2 * S), lax.rem(lax.div(c, 2), S), lax.rem(c, 2)
    sib = 1 - core

    def rid(yy, hh):
        return yy * S + hh

    def cid(xx, zz, cc):
        return (xx * S + zz) * 2 + cc

    def quarter(xx, yy):
        return mod(2 * xx + S - yy)

    mine = quarter(x, y)
    line = (z + 1 - 2 * lax.rem(z, 2), jnp.where(z < 2, 2, 1), jnp.where(z < 2, 3, 0))
    right, left, partner = cid(mod(x + 1), z, core), cid(mod(x + 3), z, core), cid(x, z, sib)
    across_x = cid(mod(x + 2), z, core)

    barrier = pltpu.get_barrier_semaphore()

    def greet(sem, rr, cc):
        pl.semaphore_signal(sem, inc=1, device_id=(rr, cc), device_id_type=MESH)

    greet(barrier, rid(y, mod(h + 1)), c)
    greet(barrier, rid(y, mod(h + 3)), c)
    for zz in line:
        greet(barrier, r, cid(x, zz, core))
    for d in (2, 1, 3):
        greet(barrier, rid(mod(y + d), h), c)
    for cc in (right, left, across_x, partner):
        greet(barrier, r, cc)

    small = [
        pltpu.make_async_copy(src, dst, i_sem.at[e])
        for e, (src, dst) in enumerate([(fac_in, fac_ref), (lst_in, lst_ref), (pat_in, pat_ref)])
    ]
    for it in small:
        it.start()
    load = pltpu.make_async_copy(inv_in, inv, i_sem.at[3])
    load.start()
    for it in small[:2]:
        it.wait()

    listed = lst_ref[...].astype(F32)
    eye = lax.broadcasted_iota(jnp.int32, (ROWS, ROWS), 0) == lax.broadcasted_iota(jnp.int32, (ROWS, ROWS), 1)
    lane = lax.broadcasted_iota(jnp.int32, (ROWS, LANES), 1)
    row = lax.broadcasted_iota(jnp.int32, (ROWS, LANES), 0)
    spot = lane == row + lax.rem(c, LANES // ROWS) * ROWS
    lines = []
    for k in range(KS):
        flag = jnp.sum(jnp.where(eye, listed[k : k + 1, :], 0.0), axis=1, keepdims=True)
        rows = regroup(fac_ref[:, k, :] * flag)
        for t in range(S):
            at = HEAD + (k * S + t) * ROWS
            gat[c, at : at + ROWS, :] = rows[:, t * LANES : (t + 1) * LANES]
        lines.append(jnp.sum(jnp.where(spot, flag, 0.0), axis=0, keepdims=True))
    which = lax.broadcasted_iota(jnp.int32, (HEAD, LANES), 0) == 0
    gat[c, :HEAD, :] = jnp.where(which, lines[0], lines[1])

    pl.semaphore_wait(barrier, 12)

    rounds = (
        [(rid(y, mod(h + 1)), c), (rid(y, mod(h + 3)), c)],
        [(rid(mod(y + d), h), c) for d in (2, 1, 3)],
        [(r, cid(x, zz, core)) for zz in line],
        [(r, right), (r, left), (r, across_x)],
        [(r, partner)],
    )

    def tell(n):
        for rr, cc in rounds[n]:
            greet(far_sem.at[n], rr, cc)

    def heard(n):
        pl.semaphore_wait(far_sem.at[n], len(rounds[n]))
        if n + 1 < len(rounds):
            tell(n + 1)

    tell(0)

    sends = []

    def copy(src, dst, ssem, rsem, rr, cc):
        return pltpu.make_async_remote_copy(
            src_ref=src, dst_ref=dst, send_sem=ssem, recv_sem=rsem, device_id=(rr, cc), device_id_type=MESH
        )

    def send(*args):
        it = copy(*args)
        it.start()
        sends.append(it)

    def arrive(dst, sem):
        pltpu.make_async_copy(dst, dst, sem).wait()

    def span(n):
        first = 0 if n == 0 else HEAD + CUTS[n] * ROWS
        return pl.ds(first, HEAD + CUTS[n + 1] * ROWS - first)

    def pass_on(n, cs, *to):
        shard = gat.at[cs, span(n)]
        for cc in to:
            copy(shard, shard, g_send.at[n], g_recv.at[n, cs], r, cc).start()

    def got(n, cs):
        arrive(gat.at[cs, span(n)], g_recv.at[n, cs])

    def start_gather(n):
        pass_on(n, c, right, left, across_x, cid(x, line[2], core), cid(x, line[1], core), cid(x, line[0], core), partner)

    def line_gather(n):
        lines = [cid(x, zz, core) for zz in line]
        rings = [left, right, across_x]
        if n in ROUND:
            for cs in rings:
                got(n, cs)
                pass_on(n, cs, *lines, partner)
            for cs in lines:
                got(n, cs)
                pass_on(n, cs, partner)
        else:
            for cs in rings[:2]:
                got(n, cs)
                pass_on(n, cs, partner)
            for cs in lines:
                got(n, cs)
                pass_on(n, cs, *rings, partner)
            got(n, across_x)
            pass_on(n, across_x, partner)

    def relay_gather(n):
        for zz in line:
            for d in (3, 1):
                cs = cid(mod(x + d), zz, core)
                got(n, cs)
                pass_on(n, cs, partner)

    def finish_gather(n):
        for zz in line:
            cs = cid(mod(x + 2), zz, core)
            got(n, cs)
            pass_on(n, cs, partner)
        for cs in range(S * S):
            got(n, 2 * cs + sib)

    def gathered(n):
        shards = gat.at[pl.ds(0, 31), span(n)]
        pltpu.make_async_copy(shards, shards, g_send.at[n]).wait()

    def prepare():
        small[2].wait()
        flags = pat_ref[...].astype(F32)
        tile = lax.div(lax.broadcasted_iota(jnp.int32, (S, 512), 1), 64)
        wide = jnp.zeros((S, 512), F32)
        for e in range(8):
            wide = jnp.where(tile == e, flags[:, e : e + 1], wide)
        load.wait()
        for g in range(4):
            at = slice(g * LANES, (g + 1) * LANES)
            mask = jnp.concatenate([jnp.broadcast_to(wide[t : t + 1, at], (64, LANES)) for t in range(S)], axis=0)
            hi, lo = split(inv[at, :].T * mask)
            ph[:, at] = hi
            plo[:, at] = lo

    def blocks(n):
        return range(CUTS[n], CUTS[n + 1])

    def product(n):
        k, p = CUTS[n] // S, CUTS[n] % S
        cols = slice(p * LANES, p * LANES + len(blocks(n)) * LANES)
        rows = [gat[:, HEAD + b * ROWS : HEAD + (b + 1) * ROWS, :].reshape(32 * ROWS, LANES) for b in blocks(n)]
        bh, bl = split(jnp.concatenate(rows, axis=1))
        mh[k, :, cols] = bh
        ml[k, :, cols] = bl
        t = dot3(ph[...], plo[...], bh, bl).T
        for e, b in enumerate(blocks(n)):
            for q in range(S):
                at = (e * S + q) * PART
                tq[q, b] = t[at : at + PART]
        run = pl.ds(CUTS[n], len(blocks(n)))
        for d in (2, 1, 3):
            yy = mod(y + d)
            send(tq.at[quarter(x, yy), run], yb.at[d, run], y_send.at[n, d], y_recv.at[n, d], rid(yy, h), c)

    def owners(n):
        for b in blocks(n):
            for cc in range(2):
                yield b, cc, rid(x, z), cid(mine, b % S, cc)

    def to_owner(n):
        run = pl.ds(CUTS[n], len(blocks(n)))
        for d in (1, 3, 2):
            arrive(yb.at[d, run], y_recv.at[n, d])
        total = (tq[mine, run] + yb[1, run]) + (yb[2, run] + yb[3, run])
        zt[run] = total.reshape(len(blocks(n)), 2, ROWS, 256)
        for b, e, rr, ct in owners(n):
            k = b // S
            here = jnp.logical_and(rr == r, ct == c)

            @pl.when(here)
            def _():
                pltpu.make_async_copy(zt.at[b, e], rb.at[k, h, core], z_recv.at[k, h, core]).start()

            @pl.when(jnp.logical_not(here))
            def _():
                copy(zt.at[b, e], rb.at[k, h, core], z_send.at[b, e], z_recv.at[k, h, core], rr, ct).start()

    def sent_to_owner(n):
        for b, e, rr, ct in owners(n):

            @pl.when(jnp.logical_or(rr != r, ct != c))
            def _():
                pltpu.make_async_copy(zt.at[b, e], zt.at[b, e], z_send.at[b, e]).wait()

    def update(k):
        marks = jnp.concatenate(
            [jnp.sum(gat[8 * b : 8 * b + 8, :HEAD, :], axis=0)[k : k + 1, :] for b in range(S)], axis=1
        )
        for hs in range(S):
            for cs in range(2):
                arrive(rb.at[k, hs, cs], z_recv.at[k, hs, cs])
        parts = rb[k]
        total = (parts[0] + parts[1]) + (parts[2] + parts[3])
        total = jnp.concatenate([total[0], total[1]], axis=1) * marks
        col_ref[:, k, :] = total
        ch, cl = split(total)
        both = jnp.dot(jnp.concatenate([ch, cl], axis=0), mh[k], preferred_element_type=F32)
        u = regroup(both[:ROWS] + (both[ROWS:] + jnp.dot(ch, ml[k], preferred_element_type=F32)))
        for q in range(S):
            ub[k, q] = u[:, q * LANES : (q + 1) * LANES]
        for d in (2, 1, 3):
            yy = mod(y + d)
            send(ub.at[k, yy], yu.at[k, d], u_send.at[k, d], u_recv.at[k, d], rid(yy, h), c)

    def across(k):
        for d in (1, 3, 2):
            arrive(yu.at[k, d], u_recv.at[k, d])
        zv[k, h] = (ub[k, y] + yu[k, 1]) + (yu[k, 2] + yu[k, 3])
        for d in (2, 1, 3):
            send(zv.at[k, h], zv.at[k, h], v_send.at[k, d], v_recv.at[k, d], rid(y, mod(h + d)), c)

    def back(k):
        for d in (1, 3, 2):
            hs = mod(h + S - d)
            arrive(zv.at[k, hs], v_recv.at[k, d])
        fw[k, y] = (zv[k, 0] + zv[k, 1]) + (zv[k, 2] + zv[k, 3])
        for d in (2, 1, 3):
            send(fw.at[k, y], fw.at[k, y], w_send.at[k, d], w_recv.at[k, d], rid(mod(y + d), h), c)

    def finish(k):
        for d in (1, 3, 2):
            ys = mod(y + S - d)
            arrive(fw.at[k, ys], w_recv.at[k, d])
        for q in range(S):
            sch_ref[:, k, q * LANES : (q + 1) * LANES] = fw[k, q]

    start_gather(0)
    start_gather(1)
    start_gather(2)
    start_gather(3)
    start_gather(4)
    prepare()
    line_gather(0)
    heard(0)
    line_gather(1)
    heard(1)
    line_gather(2)
    heard(2)
    line_gather(3)
    heard(3)
    line_gather(4)
    relay_gather(0)
    finish_gather(0)
    heard(4)
    product(0)
    relay_gather(1)
    finish_gather(1)
    product(1)
    relay_gather(2)
    finish_gather(2)
    product(2)
    relay_gather(3)
    finish_gather(3)
    product(3)
    to_owner(0)
    to_owner(1)
    relay_gather(4)
    finish_gather(4)
    product(4)
    to_owner(2)
    to_owner(3)
    to_owner(4)
    for n in range(CHUNKS):
        gathered(n)
    update(0)
    across(0)
    update(1)
    across(1)
    back(0)
    back(1)
    finish(0)
    finish(1)
    for it in sends:
        it.wait_send()
    for n in range(CHUNKS):
        sent_to_owner(n)


def local(inv_known, pattern, factor, listed, diag_inverse):
    width = diag_inverse.shape[0]
    vmem = pl.BlockSpec(memory_space=pltpu.VMEM)
    dma = pltpu.SemaphoreType.DMA
    out = jax.ShapeDtypeStruct((width, KS, 512), F32)
    sums, total = pl.pallas_call(
        kernel,
        out_shape=(out, out),
        in_specs=[pl.BlockSpec(memory_space=pl.ANY)] * 4,
        out_specs=(vmem, vmem),
        scratch_shapes=[
            pltpu.VMEM((512, 256), F32),
            pltpu.VMEM((S, 8), jnp.int32),
            pltpu.VMEM((ROWS, KS, 512), F32),
            pltpu.VMEM((KS, ROWS), jnp.int32),
            pltpu.VMEM((256, 512), BF16),
            pltpu.VMEM((256, 512), BF16),
            pltpu.VMEM((32, GR, LANES), F32),
            pltpu.VMEM((KS, 512, 512), BF16),
            pltpu.VMEM((KS, 512, 512), BF16),
            pltpu.VMEM((S, KS * S, PART, 256), F32),
            pltpu.VMEM((S, KS * S, PART, 256), F32),
            pltpu.VMEM((KS * S, 2, ROWS, 256), F32),
            pltpu.VMEM((KS, S, 2, ROWS, 256), F32),
            pltpu.VMEM((KS, S, ROWS, LANES), F32),
            pltpu.VMEM((KS, S, ROWS, LANES), F32),
            pltpu.VMEM((KS, S, ROWS, LANES), F32),
            pltpu.VMEM((KS, S, ROWS, LANES), F32),
            dma((4,)), pltpu.SemaphoreType.REGULAR((5,)),
            dma((CHUNKS,)), dma((CHUNKS, 32)),
            dma((CHUNKS, S)), dma((CHUNKS, S)),
            dma((KS * S, 2)), dma((KS, S, 2)),
            dma((KS, S)), dma((KS, S)),
            dma((KS, S)), dma((KS, S)),
            dma((KS, S)), dma((KS, S)),
        ],
        compiler_params=pltpu.CompilerParams(collective_id=0, has_side_effects=True),
    )(inv_known, pattern.T, factor, listed.T)

    def close(sums_ref, total_ref, dia_ref, col_ref, sch_ref):
        col_ref[...] = -sums_ref[...]
        sch_ref[...] = dia_ref[...] + total_ref[...]

    return pl.pallas_call(close, out_shape=(out, out), in_specs=[vmem] * 3, out_specs=(vmem, vmem))(
        sums, total, diag_inverse
    )


def solution(mesh):
    in_specs = (
        P("row", "col"),
        P("row", "col"),
        P(("row", "col"), None, None),
        P(("row", "col"), None),
        P("col", None, None),
    )
    out_specs = (P("col", None, "row"), P("col", None, None))
    return jax.shard_map(local, mesh=mesh, in_specs=in_specs, out_specs=out_specs, check_vma=False)
```

```python
import jax
import jax.numpy as jnp
from jax import lax
from jax.experimental import pallas as pl
from jax.experimental.pallas import tpu as pltpu
from jax.sharding import PartitionSpec as P

MESH = pl.DeviceIdType.MESH
F32 = jnp.float32
BF16 = jnp.bfloat16

S = 4
ROWS = 16
KS = 2
LANES = 128
PART = 32
CUTS = (0, 1, 2, 4, 6, 8)
CHUNKS = len(CUTS) - 1
ROUND = ()
HEAD = 8
GR = HEAD + KS * S * ROWS


def mod(v):
    return lax.rem(v, S)


def split(v):
    hi = v.astype(BF16)
    return hi, (v - hi.astype(F32)).astype(BF16)


def dot3(ah, al, bh, bl):
    def dot(a, b):
        return jnp.dot(a, b, preferred_element_type=F32)

    return dot(ah, bh) + (dot(ah, bl) + dot(al, bh))


def regroup(v):
    blocks = []
    for t in range(S):
        blocks += [v[:, q * LANES + t * PART : q * LANES + (t + 1) * PART] for q in range(S)]
    return jnp.concatenate(blocks, axis=1)


def kernel(
    inv_in, pat_in, fac_in, lst_in, col_ref, sch_ref,
    inv, pat_ref, fac_ref, lst_ref, ph, plo, gat, mh, ml, tq, yb, zt, rb, ub, yu, zv, fw,
    i_sem, far_sem, g_send, g_recv, y_send, y_recv, z_send, z_recv,
    u_send, u_recv, v_send, v_recv, w_send, w_recv,
):
    r, c = lax.axis_index("row"), lax.axis_index("col")
    y, h = lax.div(r, S), lax.rem(r, S)
    x, z, core = lax.div(c, 2 * S), lax.rem(lax.div(c, 2), S), lax.rem(c, 2)
    sib = 1 - core

    def rid(yy, hh):
        return yy * S + hh

    def cid(xx, zz, cc):
        return (xx * S + zz) * 2 + cc

    def quarter(xx, yy):
        return mod(2 * xx + S - yy)

    mine = quarter(x, y)
    line = (z + 1 - 2 * lax.rem(z, 2), jnp.where(z < 2, 2, 1), jnp.where(z < 2, 3, 0))
    right, left, partner = cid(mod(x + 1), z, core), cid(mod(x + 3), z, core), cid(x, z, sib)
    across_x = cid(mod(x + 2), z, core)

    barrier = pltpu.get_barrier_semaphore()

    def greet(sem, rr, cc):
        pl.semaphore_signal(sem, inc=1, device_id=(rr, cc), device_id_type=MESH)

    greet(barrier, rid(y, mod(h + 1)), c)
    greet(barrier, rid(y, mod(h + 3)), c)
    for zz in line:
        greet(barrier, r, cid(x, zz, core))
    for d in (2, 1, 3):
        greet(barrier, rid(mod(y + d), h), c)
    for cc in (right, left, across_x, partner):
        greet(barrier, r, cc)

    small = [
        pltpu.make_async_copy(src, dst, i_sem.at[e])
        for e, (src, dst) in enumerate([(fac_in, fac_ref), (lst_in, lst_ref), (pat_in, pat_ref)])
    ]
    for it in small:
        it.start()
    load = pltpu.make_async_copy(inv_in, inv, i_sem.at[3])
    load.start()
    for it in small[:2]:
        it.wait()

    listed = lst_ref[...].astype(F32)
    eye = lax.broadcasted_iota(jnp.int32, (ROWS, ROWS), 0) == lax.broadcasted_iota(jnp.int32, (ROWS, ROWS), 1)
    lane = lax.broadcasted_iota(jnp.int32, (ROWS, LANES), 1)
    row = lax.broadcasted_iota(jnp.int32, (ROWS, LANES), 0)
    spot = lane == row + lax.rem(c, LANES // ROWS) * ROWS
    lines = []
    for k in range(KS):
        flag = jnp.sum(jnp.where(eye, listed[k : k + 1, :], 0.0), axis=1, keepdims=True)
        rows = regroup(fac_ref[:, k, :] * flag)
        for t in range(S):
            at = HEAD + (k * S + t) * ROWS
            gat[c, at : at + ROWS, :] = rows[:, t * LANES : (t + 1) * LANES]
        lines.append(jnp.sum(jnp.where(spot, flag, 0.0), axis=0, keepdims=True))
    which = lax.broadcasted_iota(jnp.int32, (HEAD, LANES), 0) == 0
    gat[c, :HEAD, :] = jnp.where(which, lines[0], lines[1])

    pl.semaphore_wait(barrier, 12)

    rounds = (
        [(rid(y, mod(h + 1)), c), (rid(y, mod(h + 3)), c)],
        [(rid(mod(y + d), h), c) for d in (2, 1, 3)],
        [(r, cid(x, zz, core)) for zz in line],
        [(r, right), (r, left), (r, across_x)],
        [(r, partner)],
    )

    def tell(n):
        for rr, cc in rounds[n]:
            greet(far_sem.at[n], rr, cc)

    def heard(n):
        pl.semaphore_wait(far_sem.at[n], len(rounds[n]))
        if n + 1 < len(rounds):
            tell(n + 1)

    tell(0)

    sends = []

    def copy(src, dst, ssem, rsem, rr, cc):
        return pltpu.make_async_remote_copy(
            src_ref=src, dst_ref=dst, send_sem=ssem, recv_sem=rsem, device_id=(rr, cc), device_id_type=MESH
        )

    def send(*args):
        it = copy(*args)
        it.start()
        sends.append(it)

    def arrive(dst, sem):
        pltpu.make_async_copy(dst, dst, sem).wait()

    def span(n):
        first = 0 if n == 0 else HEAD + CUTS[n] * ROWS
        return pl.ds(first, HEAD + CUTS[n + 1] * ROWS - first)

    def pass_on(n, cs, *to):
        shard = gat.at[cs, span(n)]
        for cc in to:
            copy(shard, shard, g_send.at[n], g_recv.at[n, cs], r, cc).start()

    def got(n, cs):
        arrive(gat.at[cs, span(n)], g_recv.at[n, cs])

    def start_gather(n):
        pass_on(n, c, right, left, across_x, cid(x, line[2], core), cid(x, line[1], core), cid(x, line[0], core), partner)

    def line_gather(n):
        lines = [cid(x, zz, core) for zz in line]
        rings = [left, right, across_x]
        if n in ROUND:
            for cs in rings:
                got(n, cs)
                pass_on(n, cs, *lines, partner)
            for cs in lines:
                got(n, cs)
                pass_on(n, cs, partner)
        else:
            for cs in rings[:2]:
                got(n, cs)
                pass_on(n, cs, partner)
            for cs in lines:
                got(n, cs)
                pass_on(n, cs, *rings, partner)
            got(n, across_x)
            pass_on(n, across_x, partner)

    def relay_gather(n):
        for zz in line:
            for d in (3, 1):
                cs = cid(mod(x + d), zz, core)
                got(n, cs)
                pass_on(n, cs, partner)

    def finish_gather(n):
        for zz in line:
            cs = cid(mod(x + 2), zz, core)
            got(n, cs)
            pass_on(n, cs, partner)
        for cs in range(S * S):
            got(n, 2 * cs + sib)

    def gathered(n):
        shards = gat.at[pl.ds(0, 31), span(n)]
        pltpu.make_async_copy(shards, shards, g_send.at[n]).wait()

    def prepare():
        small[2].wait()
        flags = pat_ref[...].astype(F32)
        tile = lax.div(lax.broadcasted_iota(jnp.int32, (S, 512), 1), 64)
        wide = jnp.zeros((S, 512), F32)
        for e in range(8):
            wide = jnp.where(tile == e, flags[:, e : e + 1], wide)
        load.wait()
        for g in range(4):
            at = slice(g * LANES, (g + 1) * LANES)
            mask = jnp.concatenate([jnp.broadcast_to(wide[t : t + 1, at], (64, LANES)) for t in range(S)], axis=0)
            hi, lo = split(inv[at, :].T * mask)
            ph[:, at] = hi
            plo[:, at] = lo

    def blocks(n):
        return range(CUTS[n], CUTS[n + 1])

    def product(n):
        k, p = CUTS[n] // S, CUTS[n] % S
        cols = slice(p * LANES, p * LANES + len(blocks(n)) * LANES)
        rows = [gat[:, HEAD + b * ROWS : HEAD + (b + 1) * ROWS, :].reshape(32 * ROWS, LANES) for b in blocks(n)]
        bh, bl = split(jnp.concatenate(rows, axis=1))
        mh[k, :, cols] = bh
        ml[k, :, cols] = bl
        t = dot3(ph[...], plo[...], bh, bl).T
        for e, b in enumerate(blocks(n)):
            for q in range(S):
                at = (e * S + q) * PART
                tq[q, b] = t[at : at + PART]
        run = pl.ds(CUTS[n], len(blocks(n)))
        for d in (2, 1, 3):
            yy = mod(y + d)
            send(tq.at[quarter(x, yy), run], yb.at[d, run], y_send.at[n, d], y_recv.at[n, d], rid(yy, h), c)

    def owners(n):
        for b in blocks(n):
            for cc in range(2):
                yield b, cc, rid(x, z), cid(mine, b % S, cc)

    def to_owner(n):
        run = pl.ds(CUTS[n], len(blocks(n)))
        for d in (1, 3, 2):
            arrive(yb.at[d, run], y_recv.at[n, d])
        total = (tq[mine, run] + yb[1, run]) + (yb[2, run] + yb[3, run])
        zt[run] = total.reshape(len(blocks(n)), 2, ROWS, 256)
        for b, e, rr, ct in owners(n):
            k = b // S
            here = jnp.logical_and(rr == r, ct == c)

            @pl.when(here)
            def _():
                pltpu.make_async_copy(zt.at[b, e], rb.at[k, h, core], z_recv.at[k, h, core]).start()

            @pl.when(jnp.logical_not(here))
            def _():
                copy(zt.at[b, e], rb.at[k, h, core], z_send.at[b, e], z_recv.at[k, h, core], rr, ct).start()

    def sent_to_owner(n):
        for b, e, rr, ct in owners(n):

            @pl.when(jnp.logical_or(rr != r, ct != c))
            def _():
                pltpu.make_async_copy(zt.at[b, e], zt.at[b, e], z_send.at[b, e]).wait()

    def update(k):
        marks = jnp.concatenate(
            [jnp.sum(gat[8 * b : 8 * b + 8, :HEAD, :], axis=0)[k : k + 1, :] for b in range(S)], axis=1
        )
        for hs in range(S):
            for cs in range(2):
                arrive(rb.at[k, hs, cs], z_recv.at[k, hs, cs])
        parts = rb[k]
        total = (parts[0] + parts[1]) + (parts[2] + parts[3])
        total = jnp.concatenate([total[0], total[1]], axis=1) * marks
        col_ref[:, k, :] = total
        ch, cl = split(total)
        both = jnp.dot(jnp.concatenate([ch, cl], axis=0), mh[k], preferred_element_type=F32)
        u = regroup(both[:ROWS] + (both[ROWS:] + jnp.dot(ch, ml[k], preferred_element_type=F32)))
        for q in range(S):
            ub[k, q] = u[:, q * LANES : (q + 1) * LANES]
        for d in (2, 1, 3):
            yy = mod(y + d)
            send(ub.at[k, yy], yu.at[k, d], u_send.at[k, d], u_recv.at[k, d], rid(yy, h), c)

    def across(k):
        for d in (1, 3, 2):
            arrive(yu.at[k, d], u_recv.at[k, d])
        zv[k, h] = (ub[k, y] + yu[k, 1]) + (yu[k, 2] + yu[k, 3])
        for d in (2, 1, 3):
            send(zv.at[k, h], zv.at[k, h], v_send.at[k, d], v_recv.at[k, d], rid(y, mod(h + d)), c)

    def back(k):
        for d in (1, 3, 2):
            hs = mod(h + S - d)
            arrive(zv.at[k, hs], v_recv.at[k, d])
        fw[k, y] = (zv[k, 0] + zv[k, 1]) + (zv[k, 2] + zv[k, 3])
        for d in (2, 1, 3):
            send(fw.at[k, y], fw.at[k, y], w_send.at[k, d], w_recv.at[k, d], rid(mod(y + d), h), c)

    def finish(k):
        for d in (1, 3, 2):
            ys = mod(y + S - d)
            arrive(fw.at[k, ys], w_recv.at[k, d])
        for q in range(S):
            sch_ref[:, k, q * LANES : (q + 1) * LANES] = fw[k, q]

    start_gather(0)
    start_gather(1)
    start_gather(2)
    start_gather(3)
    start_gather(4)
    line_gather(0)
    heard(0)
    line_gather(1)
    heard(1)
    line_gather(2)
    heard(2)
    line_gather(3)
    heard(3)
    line_gather(4)
    prepare()
    relay_gather(0)
    finish_gather(0)
    heard(4)
    product(0)
    relay_gather(1)
    finish_gather(1)
    product(1)
    relay_gather(2)
    finish_gather(2)
    product(2)
    relay_gather(3)
    finish_gather(3)
    product(3)
    relay_gather(4)
    to_owner(0)
    to_owner(1)
    finish_gather(4)
    product(4)
    to_owner(2)
    to_owner(3)
    to_owner(4)
    update(0)
    across(0)
    update(1)
    across(1)
    back(0)
    back(1)
    finish(0)
    finish(1)
    for n in range(CHUNKS):
        gathered(n)
    for it in sends:
        it.wait_send()
    for n in range(CHUNKS):
        sent_to_owner(n)


def local(inv_known, pattern, factor, listed, diag_inverse):
    width = diag_inverse.shape[0]
    vmem = pl.BlockSpec(memory_space=pltpu.VMEM)
    dma = pltpu.SemaphoreType.DMA
    out = jax.ShapeDtypeStruct((width, KS, 512), F32)
    sums, total = pl.pallas_call(
        kernel,
        out_shape=(out, out),
        in_specs=[pl.BlockSpec(memory_space=pl.ANY)] * 4,
        out_specs=(vmem, vmem),
        scratch_shapes=[
            pltpu.VMEM((512, 256), F32),
            pltpu.VMEM((S, 8), jnp.int32),
            pltpu.VMEM((ROWS, KS, 512), F32),
            pltpu.VMEM((KS, ROWS), jnp.int32),
            pltpu.VMEM((256, 512), BF16),
            pltpu.VMEM((256, 512), BF16),
            pltpu.VMEM((32, GR, LANES), F32),
            pltpu.VMEM((KS, 512, 512), BF16),
            pltpu.VMEM((KS, 512, 512), BF16),
            pltpu.VMEM((S, KS * S, PART, 256), F32),
            pltpu.VMEM((S, KS * S, PART, 256), F32),
            pltpu.VMEM((KS * S, 2, ROWS, 256), F32),
            pltpu.VMEM((KS, S, 2, ROWS, 256), F32),
            pltpu.VMEM((KS, S, ROWS, LANES), F32),
            pltpu.VMEM((KS, S, ROWS, LANES), F32),
            pltpu.VMEM((KS, S, ROWS, LANES), F32),
            pltpu.VMEM((KS, S, ROWS, LANES), F32),
            dma((4,)), pltpu.SemaphoreType.REGULAR((5,)),
            dma((CHUNKS,)), dma((CHUNKS, 32)),
            dma((CHUNKS, S)), dma((CHUNKS, S)),
            dma((KS * S, 2)), dma((KS, S, 2)),
            dma((KS, S)), dma((KS, S)),
            dma((KS, S)), dma((KS, S)),
            dma((KS, S)), dma((KS, S)),
        ],
        compiler_params=pltpu.CompilerParams(collective_id=0, has_side_effects=True),
    )(inv_known, pattern.T, factor, listed.T)

    def close(sums_ref, total_ref, dia_ref, col_ref, sch_ref):
        col_ref[...] = -sums_ref[...]
        sch_ref[...] = dia_ref[...] + total_ref[...]

    return pl.pallas_call(close, out_shape=(out, out), in_specs=[vmem] * 3, out_specs=(vmem, vmem))(
        sums, total, diag_inverse
    )


def solution(mesh):
    in_specs = (
        P("row", "col"),
        P("row", "col"),
        P(("row", "col"), None, None),
        P(("row", "col"), None),
        P("col", None, None),
    )
    out_specs = (P("col", None, "row"), P("col", None, None))
    return jax.shard_map(local, mesh=mesh, in_specs=in_specs, out_specs=out_specs, check_vma=False)
```
